128 devices in a mesh: dp: 8 (over x, core), fsdp: 16 (over z, y).
Axes of the slice: x: 4, y: 4, z: 4, core: 2. Of those that a mesh axis runs over, the one named last changes fastest.
Arguments:
- q_inputs: bfloat16 [131072, 768], P(('dp', 'fsdp')), may hold values from -6 to 6
- q_grads: bfloat16 [131072, 6144], P(('dp', 'fsdp')), may hold values from -0.15625 to 0.15625
- k_inputs: bfloat16 [131072, 512], P(('dp', 'fsdp')), may hold values from -6 to 6
- k_grads: bfloat16 [131072, 4096], P(('dp', 'fsdp')), may hold values from -0.15625 to 0.15625
- q_master: float32 [6144, 768], P(('dp', 'fsdp')), may hold values from -3 to 3
- k_master: float32 [4096, 512], P(('dp', 'fsdp')), may hold values from -3 to 3
- q_momentum: float32 [6144, 768], P(('dp', 'fsdp')), may hold values from -25 to 25, as said below
- k_momentum: float32 [4096, 512], P(('dp', 'fsdp')), may hold values from -25 to 25, as said below
- logit_peaks: float32 [128, 32], P(('dp', 'fsdp')), may hold values from 10 to 500, as said below
- clip_flags: int32 [2, 32], replicated, may hold values 0 or 1
Outputs:
- new_q_master: float32 [6144, 768], P(('dp', 'fsdp'))
- new_k_master: float32 [4096, 512], P(('dp', 'fsdp'))
- new_q_momentum: float32 [6144, 768], P(('dp', 'fsdp'))
- new_k_momentum: float32 [4096, 512], P(('dp', 'fsdp'))
- q_weights: bfloat16 [6144, 768], P('dp')
- k_weights: bfloat16 [4096, 512], P('dp')
The draws below stay inside these ranges and needn't reach their ends.
Inputs may be any that keep to these rules, and one draw needn't show every extreme that they name: `q_momentum`: the momenta are finite reals of mixed sign. `k_momentum`: the momenta are finite reals of mixed sign. `logit_peaks`: every entry is positive.
All inputs are finite; a program needn't handle non-finite values.
Results may differ from the reference program's by a relative error of at most 0.0004.
Values may be sent and summed in bfloat16 or wider, within the bound.
No kernel may reach another device: no remote copies, remote signals or barrier semaphores. Data moves between devices by JAX's collectives and lax.ppermute only.
A program may use at most 128 MiB of HBM per device.

```python
import math
import jax
import jax.numpy as jnp
from jax import lax

QR = 768
KR = 512
HEADS = 32
QNOPE = 128
QROPE = 64
NS_ITERS = 3
TOK_DEV = 1024
SHARDS = 128
TOKENS = 131072
QC = 6144
KC = 4096


LOGIT_CAP = 100.0


def momentum_field(key, height, breadth):
    keys = jax.random.split(key, 4)
    row_scale = jnp.exp(jax.random.uniform(keys[0], (height, 1), jnp.float32) * math.log(10.0))
    col_scale = jnp.exp(jax.random.uniform(keys[1], (1, breadth), jnp.float32) * math.log(3.0))
    rising = 1.0 + 2.0 * jnp.arange(height, dtype=jnp.float32)[:, None] / height
    base = jnp.clip(jax.random.normal(keys[2], (height, breadth), jnp.float32), -4.0, 4.0)
    core = (base + 0.7 * jnp.roll(base, 1, axis=1)) / math.sqrt(1.49)
    return core * row_scale * col_scale * rising * 0.05


def draw_q_momentum(key, part):
    return momentum_field(jax.random.fold_in(key, 11), QC, QR)


def draw_k_momentum(key, part):
    return momentum_field(jax.random.fold_in(key, 12), KC, KR)


def draw_logit_peaks(key, part):
    keys = jax.random.split(jax.random.fold_in(key, 13), 3)
    rising = 1.0 + 2.0 * jnp.arange(SHARDS, dtype=jnp.float32)[:, None] / max(SHARDS - 1, 1)
    spread = jax.random.uniform(keys[0], (SHARDS, HEADS), jnp.float32)
    base = LOGIT_CAP * (0.1 + 0.15 * spread) * rising
    owner = jax.random.randint(keys[1], (1, HEADS), 0, SHARDS)
    peak = LOGIT_CAP * (0.6 + 4.4 * jax.random.uniform(keys[2], (1, HEADS), jnp.float32))
    hit = jnp.arange(SHARDS, dtype=jnp.int32)[:, None] == owner
    return jnp.where(hit, jnp.maximum(peak, base), base)


def plant(values, own_key, least, top_value):
    longest = values.shape.index(max(values.shape))
    spots = []
    for shift in (0, 1):
        where = [jax.random.randint(jax.random.fold_in(own_key, axis), (), 0, length) for axis, length in enumerate(values.shape)]
        where[longest] = (where[longest] + shift) % values.shape[longest]
        spots.append(tuple(where))
    return values.at[spots[0]].set(least).at[spots[1]].set(top_value)


def strengthened(values, own_key, source, target, parts, factor):
    def block_of(dim):
        return (jnp.arange(values.shape[dim]) // (values.shape[dim] // parts)).reshape((-1,) + (1,) * (values.ndim - 1 - dim))

    first = jax.random.permutation(own_key, parts)[block_of(target)]
    second = (block_of(target) + parts // 2) % parts
    return jnp.where((block_of(source) == first) | (block_of(source) == second), factor * values, values)


def block_levels(stream_key, shape, cuts, smallest, largest):
    gain, own = 1.0, jax.random.fold_in(stream_key, 6)
    for axis_at, blocks in cuts:
        steps = jnp.exp(jax.random.uniform(jax.random.fold_in(own, axis_at), (blocks,), jnp.float32, smallest / len(cuts), largest / len(cuts)))
        gain = gain * jnp.repeat(steps, shape[axis_at] // blocks).reshape([-1 if axis == axis_at else 1 for axis in range(len(shape))])
    return gain


def scatter_about(rng, shape, deviation, reach, pieces=(), kind=jnp.bfloat16):
    factor_of = block_levels(rng, shape, pieces, -0.22, 0.18) if pieces else 1.0
    result = jax.random.normal(rng, shape, jnp.float32) * deviation * factor_of
    return jnp.minimum(jnp.maximum(result, -reach), reach).astype(kind)


def gaussian_with(own_key, dims, scale, most, cuts, heavy, kind=jnp.bfloat16):
    entries = scale * jax.random.normal(own_key, dims, jnp.float32)
    if cuts:
        entries = entries * block_levels(own_key, dims, cuts, -0.22, 0.18)
    return jnp.clip(strengthened(entries, jax.random.fold_in(own_key, 3), *heavy), -most, most).astype(kind)


def setup_inputs(seed: int = 0) -> dict:
    seeds = jax.random.split(jax.random.key(seed), 11)
    q_inputs = scatter_about(seeds[0], (TOKENS, QR), 1.0, 6.0, ((0, 128),))
    q_grads = gaussian_with(seeds[1], (TOKENS, QC), (TOKENS ** -0.5), 0.15625, ((0, 128),), (0, 1, 128, 5.5))
    k_inputs = scatter_about(seeds[2], (TOKENS, KR), 1.0, 6.0, ((0, 128),))
    k_grads = gaussian_with(seeds[3], (TOKENS, KC), (TOKENS ** -0.5), 0.15625, ((0, 128),), (0, 1, 128, 5.5))
    q_master = scatter_about(seeds[4], (QC, QR), 0.5, 3.0, ((0, 128),), jnp.float32)
    k_master = scatter_about(seeds[5], (KC, KR), 0.5, 3.0, ((0, 128),), jnp.float32)
    q_momentum = draw_q_momentum(jax.random.fold_in(seeds[10], 71), 0)
    k_momentum = draw_k_momentum(jax.random.fold_in(seeds[10], 71), 0)
    logit_peaks = draw_logit_peaks(jax.random.fold_in(seeds[10], 71), 0)
    clip_flags = plant((jax.random.randint(seeds[9], (2, HEADS), 0, 4) < 3).astype(jnp.int32), jax.random.fold_in(seeds[9], 1), 0, 1)
    return {"q_inputs": q_inputs, "q_grads": q_grads, "k_inputs": k_inputs, "k_grads": k_grads, "q_master": q_master, "k_master": k_master, "q_momentum": q_momentum, "k_momentum": k_momentum, "logit_peaks": logit_peaks, "clip_flags": clip_flags}


COEF_A = 3.4445
COEF_B = -4.775
COEF_C = 2.0315
MOMENTUM_RATE = 0.95
STEP_SIZE = 0.5
DECAY_RATE = 0.1
LOGIT_CAP = 100.0
NORM_EPS = 1e-07
HIGH = lax.Precision.HIGHEST

def weight_gradient(inputs, grads):
    blocks = inputs.shape[0] // TOK_DEV
    input_blocks = inputs.reshape(blocks, TOK_DEV, inputs.shape[1])
    grad_blocks = grads.reshape(blocks, TOK_DEV, grads.shape[1])

    def add_block(running, operands):
        input_block = operands[0].astype(jnp.float32)
        grad_block = operands[1].astype(jnp.float32)
        term = lax.dot_general(grad_block, input_block, (((0,), (0,)), ((), ())), precision=HIGH, preferred_element_type=jnp.float32)
        return (running + term, None)
    initial = jnp.zeros((grads.shape[1], inputs.shape[1]), jnp.float32)
    running, unused = lax.scan(add_block, initial, (input_blocks, grad_blocks))
    return running

def orthogonalize(moment):
    norm_value = jnp.sqrt(jnp.sum(moment * moment))
    current = moment / (norm_value + NORM_EPS)
    for iteration in range(NS_ITERS):
        gram = lax.dot_general(current, current, (((0,), (0,)), ((), ())), precision=HIGH, preferred_element_type=jnp.float32)
        mixed = COEF_B * gram + COEF_C * jnp.dot(gram, gram, precision=HIGH, preferred_element_type=jnp.float32)
        current = COEF_A * current + jnp.dot(current, mixed, precision=HIGH, preferred_element_type=jnp.float32)
    return current

def reference(q_inputs, q_grads, k_inputs, k_grads, q_master, k_master, q_momentum, k_momentum, logit_peaks, clip_flags):
    new_q_momentum = MOMENTUM_RATE * q_momentum + weight_gradient(q_inputs, q_grads)
    new_k_momentum = MOMENTUM_RATE * k_momentum + weight_gradient(k_inputs, k_grads)
    q_ortho = orthogonalize(new_q_momentum)
    k_ortho = orthogonalize(new_k_momentum)
    peaks = lax.optimization_barrier(jnp.max(logit_peaks, axis=0))
    ratio = jnp.minimum(1.0, LOGIT_CAP / peaks)
    root = jnp.sqrt(ratio)
    head_span = QNOPE + QROPE
    q_ids = jnp.arange(QC, dtype=jnp.int32)
    q_head = q_ids // head_span
    q_nope = q_ids % head_span < QNOPE
    q_flag = clip_flags[0] == 1
    q_factor = jnp.where(q_flag[q_head], jnp.where(q_nope, root[q_head], ratio[q_head]), 1.0)
    k_ids = jnp.arange(KC, dtype=jnp.int32)
    k_head = k_ids // QNOPE
    k_flag = clip_flags[1] == 1
    k_factor = jnp.where(k_flag[k_head], root[k_head], 1.0)
    q_gain = 0.2 * math.sqrt(max(QC, QR))
    k_gain = 0.2 * math.sqrt(max(KC, KR))
    new_q_master = (q_master - STEP_SIZE * (q_gain * q_ortho + DECAY_RATE * q_master)) * q_factor[:, None]
    new_k_master = (k_master - STEP_SIZE * (k_gain * k_ortho + DECAY_RATE * k_master)) * k_factor[:, None]
    return (new_q_master, new_k_master, new_q_momentum, new_k_momentum, new_q_master.astype(jnp.bfloat16), new_k_master.astype(jnp.bfloat16))
```

```python
import math

import jax
import jax.numpy as jnp
from jax import lax
from jax.sharding import PartitionSpec as P

QNOPE = 128
QROPE = 64
NS_ITERS = 3


COEF_A = 3.4445
COEF_B = -4.775
COEF_C = 2.0315
MOMENTUM_RATE = 0.95
STEP_SIZE = 0.5
DECAY_RATE = 0.1
LOGIT_CAP = 100.0
NORM_EPS = 1e-07
HIGH = lax.Precision.HIGH


def hdot(first, second):
    return jnp.dot(first, second, precision=HIGH, preferred_element_type=jnp.float32)


def gram(current):
    return lax.dot_general(
        current,
        current,
        (((0,), (0,)), ((), ())),
        precision=HIGH,
        preferred_element_type=jnp.float32,
    )


def gram_pair(first, second):
    return lax.psum((gram(first), gram(second)), ("dp", "fsdp"))


def column_terms(grads, inputs):
    return lax.dot_general(
        grads, inputs, (((0,), (0,)), ((), ())), preferred_element_type=jnp.float32
    )


def orthogonalize(moment, moment_gram):
    scale = 1.0 / (jnp.sqrt(jnp.trace(moment_gram)) + NORM_EPS)
    current = moment * scale
    gram_now = moment_gram * scale * scale
    eye = jnp.eye(gram_now.shape[0], dtype=jnp.float32)
    for iteration in range(NS_ITERS):
        if iteration == NS_ITERS - 1:
            inner = COEF_B * current + COEF_C * hdot(current, gram_now)
            return COEF_A * current + hdot(inner, gram_now)
        mixed = COEF_B * gram_now + COEF_C * hdot(gram_now, gram_now)
        current = COEF_A * current + hdot(current, mixed)
        step = COEF_A * eye + mixed
        gram_now = hdot(hdot(gram_now, step), step)


def row_factors(row_ids, head_span, nope_width, flags, ratio, root, heads):
    head_ids = row_ids // head_span
    is_nope = row_ids % head_span < nope_width
    chosen = flags == 1
    nope_value = jnp.where(chosen, root, 1.0)
    rope_value = jnp.where(chosen, ratio, 1.0)
    onehot = (head_ids[:, None] == lax.iota(jnp.int32, heads)[None, :]).astype(jnp.float32)
    values = jnp.where(is_nope[:, None], nope_value[None, :], rope_value[None, :])
    return jnp.sum(onehot * values, axis=1)


def body(
    q_inputs,
    q_grads,
    k_inputs,
    k_grads,
    q_master,
    k_master,
    q_momentum,
    k_momentum,
    logit_peaks,
    clip_flags,
):
    shards = lax.axis_size(("dp", "fsdp"))
    q_rows = q_master.shape[0]
    k_rows = k_master.shape[0]
    q_terms = column_terms(q_grads, q_inputs).reshape(shards, q_rows, -1)
    k_terms = column_terms(k_grads, k_inputs).reshape(shards, k_rows, -1)
    k_terms = jnp.pad(k_terms, ((0, 0), (0, q_rows - k_rows), (0, 0)))
    both = lax.psum_scatter(
        jnp.concatenate((q_terms, k_terms), axis=2),
        ("dp", "fsdp"),
        scatter_dimension=0,
        tiled=True,
    )[0]
    q_grad = both[:, : q_master.shape[1]]
    k_grad = both[:k_rows, q_master.shape[1] :]
    new_q_momentum = MOMENTUM_RATE * q_momentum + q_grad
    new_k_momentum = MOMENTUM_RATE * k_momentum + k_grad
    q_gram, k_gram = gram_pair(new_q_momentum, new_k_momentum)
    q_iterate = orthogonalize(new_q_momentum, q_gram)
    k_iterate = orthogonalize(new_k_momentum, k_gram)
    peaks = lax.pmax(lax.pmax(logit_peaks[0], "dp"), "fsdp")
    ratio = jnp.minimum(1.0, LOGIT_CAP / peaks)
    root = jnp.sqrt(ratio)
    heads = logit_peaks.shape[1]
    block = lax.axis_index(("dp", "fsdp"))
    q_ids = block * q_rows + lax.iota(jnp.int32, q_rows)
    k_ids = block * k_rows + lax.iota(jnp.int32, k_rows)
    q_factor = row_factors(q_ids, QNOPE + QROPE, QNOPE, clip_flags[0], ratio, root, heads)
    k_factor = row_factors(k_ids, QNOPE, QNOPE, clip_flags[1], ratio, root, heads)
    q_gain = 0.2 * math.sqrt(max(shards * q_rows, q_master.shape[1]))
    k_gain = 0.2 * math.sqrt(max(shards * k_rows, k_master.shape[1]))
    new_q_master = (q_master - STEP_SIZE * (q_gain * q_iterate + DECAY_RATE * q_master)) * q_factor[
        :, None
    ]
    new_k_master = (k_master - STEP_SIZE * (k_gain * k_iterate + DECAY_RATE * k_master)) * k_factor[
        :, None
    ]
    q_weights, k_weights = (
        lax.all_gather(new_q_master.astype(jnp.bfloat16), "fsdp", axis=0, tiled=True),
        lax.all_gather(new_k_master.astype(jnp.bfloat16), "fsdp", axis=0, tiled=True),
    )
    return (new_q_master, new_k_master, new_q_momentum, new_k_momentum, q_weights, k_weights)


def solution(mesh):
    placed = (
        P(("dp", "fsdp"), None),
        P(("dp", "fsdp"), None),
        P(("dp", "fsdp"), None),
        P(("dp", "fsdp"), None),
        P(("dp", "fsdp"), None),
        P(("dp", "fsdp"), None),
        P(("dp", "fsdp"), None),
        P(("dp", "fsdp"), None),
        P(("dp", "fsdp"), None),
        P(),
    )
    return jax.shard_map(
        body,
        mesh=mesh,
        in_specs=placed,
        out_specs=(
            P(("dp", "fsdp"), None),
            P(("dp", "fsdp"), None),
            P(("dp", "fsdp"), None),
            P(("dp", "fsdp"), None),
            P("dp", None),
            P("dp", None),
        ),
        check_vma=False,
    )
```

```python
import functools
import math

import jax
import jax.numpy as jnp
from jax import lax
from jax.experimental import pallas as pl
from jax.experimental.pallas import tpu as pltpu
from jax.sharding import PartitionSpec as P

QNOPE = 128
QROPE = 64
NS_ITERS = 3


COEF_A = 3.4445
COEF_B = -4.775
COEF_C = 2.0315
MOMENTUM_RATE = 0.95
STEP_SIZE = 0.5
DECAY_RATE = 0.1
LOGIT_CAP = 100.0
NORM_EPS = 1e-07

AXES = ("dp", "fsdp")
F32 = jnp.float32
BF16 = jnp.bfloat16
SIZES = {"x": 4, "core": 2, "z": 4, "y": 4}
STRIDES = {"x": 32, "core": 16, "z": 4, "y": 1}
ORDERS = (("x", "z", "y"), ("y", "x", "z"), ("z", "y", "x"))
WIDE = 256
LANES = 128
WIRE_SCALE = 32.0


def hop(array, axis, distance):
    size, stride = SIZES[axis], STRIDES[axis]
    pairs = []
    for source in range(128):
        at = source // stride % size
        pairs.append((source, source + ((at + distance) % size - at) * stride))
    return lax.ppermute(array, AXES, pairs)


def whole(shape):
    return pl.BlockSpec(shape, lambda *_: (0,) * len(shape))


def terms(q_grads, k_grads, q_inputs, k_inputs):
    contract = (((0,), (0,)), ((), ()))
    return (
        lax.dot_general(q_grads[...], q_inputs[...], contract, preferred_element_type=F32),
        lax.dot_general(k_grads[...], k_inputs[...], contract, preferred_element_type=F32),
    )


def send_kernel(k_from, k_count, position, q_grads, k_grads, q_inputs, k_inputs, out):
    q_terms, k_terms = terms(q_grads, k_grads, q_inputs, k_inputs)
    q_rows, k_rows = q_terms.shape[0] // 16, k_terms.shape[0] // 16
    for z in range(4):
        for y in range(4):
            slot = (z + 4 - position[2]) % 4 * 4 + (y + 4 - position[3]) % 4
            q_at, k_at = (z * 4 + y) * q_rows, (z * 4 + y) * k_rows + k_from
            out[0, slot, :q_rows] = q_terms[q_at : q_at + q_rows]
            out[0, slot, q_rows:] = k_terms[k_at : k_at + k_count]


def keep_kernel(
    color,
    k_from,
    k_count,
    position,
    q_grads,
    k_grads,
    q_inputs,
    k_inputs,
    arrived,
    own,
    first,
    second,
    third,
    q_held,
    k_held,
):
    q_terms, k_terms = terms(q_grads, k_grads, q_inputs, k_inputs)
    q_rows, k_rows = q_terms.shape[0] // 16, k_terms.shape[0] // 16
    for n in range(16):
        q_held[n] = q_terms[n * q_rows : (n + 1) * q_rows]
        k_held[n] = k_terms[n * k_rows + k_from : n * k_rows + k_from + k_count]

    def store(out, at, slot, z, y):
        source = (z + position[2]) % 4 * 4 + (y + position[3]) % 4
        q_value = q_held[source] + arrived[0, slot, :q_rows]
        k_value = k_held[source] + arrived[0, slot, q_rows:]
        out[at[0], at[1], :q_rows] = q_value
        out[at[0], at[1], q_rows:] = k_value

    outs = (own, first, second, third)
    if color == 0:
        for x in range(4):

            @pl.when(pl.program_id(0) == x)
            def _(out=outs[x]):
                for z in range(4):
                    for y in range(4):
                        store(out, (z, y), z * 4 + y, z, y)
    else:
        for z in range(4):
            for y in range(4):
                if color == 1:
                    store(outs[y], (0, z), z * 4 + y, z, y)
                else:
                    store(outs[z], (y, 0), z * 4 + y, z, y)


def gradient_terms(position, color, core_step, operands, arrived=None):
    q_grads, k_grads, q_inputs, k_inputs = operands
    tokens = q_grads.shape[0]
    q_slab, k_slab = q_grads.shape[1] // 8, k_grads.shape[1] // 8
    q_rows, k_rows = q_slab // 16, k_slab // 16
    q_at, k_at = (2, 1) if color == 0 else (color - 1, 0)
    k_from, k_count = (0, k_rows) if color == 0 else ((color - 1) * k_rows // 2, k_rows // 2)
    height = q_rows + k_count

    def slab(step, position):
        return (0, (position[0] + step) % 4 * 2 + (position[1] + core_step) % 2)

    in_specs = [
        pl.BlockSpec((tokens, q_slab), slab),
        pl.BlockSpec((tokens, k_slab), slab),
        pl.BlockSpec((tokens, WIDE), lambda step, position: (0, q_at)),
        pl.BlockSpec((tokens, WIDE), lambda step, position: (0, k_at)),
    ]
    flops = 2 * tokens * 4 * WIDE * (q_slab + k_slab)
    moved = 2 * tokens * 4 * (q_slab + k_slab) + 4 * 64 * height * WIDE
    by_slab = pl.BlockSpec((1, 16, height, WIDE), lambda step, position: (step, 0, 0, 0))
    if arrived is None:
        kernel = functools.partial(send_kernel, k_from, k_count)
        out_specs, scratch, inputs = [by_slab], [], operands
        out_shape = [jax.ShapeDtypeStruct((4, 16, height, WIDE), F32)]
    else:
        kernel = functools.partial(keep_kernel, color, k_from, k_count)
        in_specs = in_specs + [by_slab]
        inputs = operands + (arrived,)
        block, index = (
            ((4, 4, height, WIDE), lambda step, position: (0, 0, 0, 0)),
            ((1, 4, height, WIDE), lambda step, position: (step, 0, 0, 0)),
            ((4, 1, height, WIDE), lambda step, position: (0, step, 0, 0)),
        )[color]
        out_specs = [pl.BlockSpec(block, index)] * 4
        out_shape = [
            jax.ShapeDtypeStruct((4, 4, height, WIDE), F32)
        ] * 4
        scratch = [pltpu.VMEM((16, q_rows, WIDE), F32), pltpu.VMEM((16, k_count, WIDE), F32)]
        moved += 4 * 64 * height * WIDE
    return pl.pallas_call(
        kernel,
        grid_spec=pltpu.PrefetchScalarGridSpec(
            num_scalar_prefetch=1,
            grid=(4,),
            in_specs=in_specs,
            out_specs=out_specs,
            scratch_shapes=scratch,
        ),
        out_shape=out_shape,
        cost_estimate=pl.CostEstimate(flops=flops, bytes_accessed=moved, transcendentals=0),
        compiler_params=pltpu.CompilerParams(vmem_limit_bytes=40 << 20),
    )(position, *inputs)


def send_all(held, stage):
    arrived = [[parts[0]] for parts in held]
    for distance in (1, 2, 3):
        for color, parts in enumerate(held):
            part, axis = parts[distance], ORDERS[color][stage]
            if stage == 0:
                part = hop((part * WIRE_SCALE).astype(jnp.float16), axis, distance)
            else:
                part = hop(part, axis, distance)
            arrived[color].append(part)
    arrived = lax.optimization_barrier(arrived)
    if stage == 0:
        arrived = [
            parts[:1] + [part.astype(F32) * (1.0 / WIRE_SCALE) for part in parts[1:]]
            for parts in arrived
        ]
    return arrived


def next_parts(arrived):
    held = []
    for parts in arrived:
        total = parts[0] + (parts[1] + parts[2] + parts[3])
        held.append([total[d] for d in range(4)])
    return held


def split(value):
    high = value.astype(BF16)
    return high, (value - high.astype(F32)).astype(BF16)


def dot3(first, second, contract=(((1,), (0,)), ((), ()))):
    def one(a, b):
        return lax.dot_general(a, b, contract, preferred_element_type=F32)

    return one(first[0], second[0]) + (one(first[0], second[1]) + one(first[1], second[0]))


def gram_kernel(*refs):
    q_momentum, k_momentum, peaks, new_q, new_k, packed = refs[12:]
    zero, one, two = (
        refs[n][...] + refs[n + 1][...] + refs[n + 2][...] + refs[n + 3][...] for n in (0, 4, 8)
    )
    q_rows, k_rows = q_momentum.shape[0], k_momentum.shape[0]
    half = k_rows // 2
    for n, color in enumerate((one, two, zero)):
        cols = slice(n * WIDE, (n + 1) * WIDE)
        new_q[:, cols] = MOMENTUM_RATE * q_momentum[:, cols] + color[:q_rows]
    new_k[:half, :WIDE] = MOMENTUM_RATE * k_momentum[:half, :WIDE] + one[q_rows:]
    new_k[half:, :WIDE] = MOMENTUM_RATE * k_momentum[half:, :WIDE] + two[q_rows:]
    new_k[:, WIDE:] = MOMENTUM_RATE * k_momentum[:, WIDE:] + zero[q_rows:]
    block = 0
    for moment in (new_q, new_k):
        high, low = split(moment[...])
        count = moment.shape[1] // LANES
        for i in range(count):
            rows = slice(i * LANES, (i + 1) * LANES)
            product = dot3(
                (high[:, rows], low[:, rows]),
                (high[:, i * LANES :], low[:, i * LANES :]),
                (((0,), (0,)), ((), ())),
            )
            for j in range(count - i):
                packed[block] = product[:, j * LANES : (j + 1) * LANES]
                block += 1
    packed[block] = jnp.broadcast_to(peaks[...], (LANES, LANES))


def orthogonal(packed, first, moment, gram, poly, temp):
    size = gram.shape[1]
    count = size // LANES
    trace = jnp.zeros((1, 1), F32)
    diagonal = lax.broadcasted_iota(jnp.int32, (LANES, LANES), 0) == lax.broadcasted_iota(
        jnp.int32, (LANES, LANES), 1
    )
    block = first
    for i in range(count):
        held = jnp.where(diagonal, packed[block], 0.0)
        trace = trace + jnp.sum(jnp.sum(held, axis=1, keepdims=True), axis=0, keepdims=True)
        block += count - i
    scale = 1.0 / (jnp.sqrt(trace) + NORM_EPS)
    square = scale * scale
    block = first
    for i in range(count):
        for j in range(i, count):
            value = packed[block] * square
            block += 1
            rows, cols = slice(i * LANES, (i + 1) * LANES), slice(j * LANES, (j + 1) * LANES)
            gram[0, rows, cols], gram[1, rows, cols] = split(value)
            if j > i:
                gram[0, cols, rows], gram[1, cols, rows] = split(value.T)

    def pair(matrix, rows=slice(None)):
        return matrix[0, rows, :], matrix[1, rows, :]

    def tiles(body):
        def step(index, carry):
            body(pl.ds(pl.multiple_of(index * WIDE, WIDE), WIDE), index * WIDE)
            return carry

        lax.fori_loop(0, size // WIDE, step, 0)

    def polynomial(rows, start):
        held = pair(gram, rows)
        row_ids = lax.broadcasted_iota(jnp.int32, (WIDE, size), 0) + start
        eye = jnp.where(row_ids == lax.broadcasted_iota(jnp.int32, (WIDE, size), 1), COEF_A, 0.0)
        value = held[0].astype(F32) + held[1].astype(F32)
        out = eye + COEF_B * value + COEF_C * dot3(held, pair(gram))
        poly[0, rows, :], poly[1, rows, :] = split(out)

    def gram_poly(rows, start):
        temp[0, rows, :], temp[1, rows, :] = split(dot3(pair(gram, rows), pair(poly)))

    def next_gram(rows, start):
        gram[0, rows, :], gram[1, rows, :] = split(dot3(pair(temp, rows), pair(poly)))

    def times(value, matrix):
        return dot3(split(value), pair(matrix))

    current = moment * scale
    tiles(polynomial)
    current = times(current, poly)
    tiles(gram_poly)
    tiles(next_gram)
    tiles(polynomial)
    current = times(current, poly)

    def last_gram(value):
        return times(times(times(value, poly), gram), poly)

    inner = COEF_B * current + COEF_C * last_gram(current)
    return COEF_A * current + last_gram(inner)


def update_kernel(
    place,
    flags,
    packed,
    new_q,
    new_k,
    q_master,
    k_master,
    new_q_master,
    new_k_master,
    weights,
    q_gram,
    q_poly,
    q_temp,
    k_gram,
    k_poly,
    k_temp,
):
    shards = 128
    block = place[0]
    q_rows, k_rows = new_q.shape[0], new_k.shape[0]
    q_blocks = (QNOPE + QROPE) // q_rows
    k_blocks = QNOPE // k_rows
    lane = lax.broadcasted_iota(jnp.int32, (1, LANES), 1)
    peaks = packed[packed.shape[0] - 1, 0:1, :]

    def ratio_of(head):
        peak = jnp.sum(jnp.where(lane == head, peaks, 0.0), axis=1, keepdims=True)
        return jnp.minimum(1.0, LOGIT_CAP / peak)

    q_head, k_head = block // q_blocks, block // k_blocks
    q_ratio, k_ratio = ratio_of(q_head), ratio_of(k_head)
    in_head = block % q_blocks * q_rows + lax.broadcasted_iota(jnp.int32, (q_rows, 1), 0)
    q_factor = jnp.where(in_head < QNOPE, jnp.sqrt(q_ratio), q_ratio)
    q_factor = jnp.where(flags[0, q_head] == 1, q_factor, 1.0)
    k_factor = jnp.where(flags[1, k_head] == 1, jnp.sqrt(k_ratio), 1.0)
    q_gain = 0.2 * math.sqrt(max(shards * q_rows, new_q.shape[1]))
    k_gain = 0.2 * math.sqrt(max(shards * k_rows, new_k.shape[1]))

    count = new_q.shape[1] // LANES
    k_ortho = orthogonal(packed, count * (count + 1) // 2, new_k[...], k_gram, k_poly, k_temp)
    k_out = (k_master[...] - STEP_SIZE * (k_gain * k_ortho + DECAY_RATE * k_master[...])) * k_factor
    new_k_master[...] = k_out
    q_ortho = orthogonal(packed, 0, new_q[...], q_gram, q_poly, q_temp)
    q_out = (q_master[...] - STEP_SIZE * (q_gain * q_ortho + DECAY_RATE * q_master[...])) * q_factor
    new_q_master[...] = q_out
    at = 0
    for value in (q_out, k_out):
        rows = value.shape[0]
        for n in range(value.shape[1] // WIDE):
            weights[at : at + rows] = value[:, n * WIDE : (n + 1) * WIDE].astype(BF16)
            at += rows


def body(
    q_inputs,
    q_grads,
    k_inputs,
    k_grads,
    q_master,
    k_master,
    q_momentum,
    k_momentum,
    logit_peaks,
    clip_flags,
):
    q_rows, q_cols = q_master.shape
    k_rows, k_cols = k_master.shape
    heads = logit_peaks.shape[1]
    dp, fsdp = lax.axis_index("dp"), lax.axis_index("fsdp")
    position = jnp.stack((dp // 2, dp % 2, fsdp // 4, fsdp % 4)).astype(jnp.int32)
    operands = (q_grads, k_grads, q_inputs, k_inputs)

    sent = [gradient_terms(position, color, 1, operands)[0] for color in range(3)]
    held = [
        gradient_terms(position, color, 0, operands, hop(sent[color], "core", 1))
        for color in range(3)
    ]
    held = next_parts(send_all(held, 0))
    held = next_parts(send_all(held, 1))
    colors = [part for parts in send_all(held, 2) for part in parts]

    q_count, k_count = q_cols // LANES, k_cols // LANES
    blocks = q_count * (q_count + 1) // 2 + k_count * (k_count + 1) // 2 + 1
    packed_shape = (blocks, LANES, LANES)
    peaks = jnp.pad(logit_peaks, ((0, 0), (0, LANES - heads)))
    smem = pl.BlockSpec(memory_space=pltpu.SMEM)
    vmem = pl.BlockSpec(memory_space=pltpu.VMEM)
    new_q_momentum, new_k_momentum, packed = pl.pallas_call(
        gram_kernel,
        in_specs=[vmem] * 15,
        out_specs=[vmem] * 3,
        out_shape=[
            jax.ShapeDtypeStruct(q_momentum.shape, F32),
            jax.ShapeDtypeStruct(k_momentum.shape, F32),
            jax.ShapeDtypeStruct(packed_shape, F32),
        ],
    )(*colors, q_momentum, k_momentum, peaks)

    shards = 128
    piece = blocks * LANES // shards
    pieces = lax.all_to_all(packed.reshape(shards, piece, LANES), AXES, 0, 0)
    block = dp * 16 + fsdp
    piece_is_peaks = block >= shards - LANES // piece
    piece_sum = jnp.where(piece_is_peaks, jnp.max(pieces, axis=0), jnp.sum(pieces, axis=0))
    packed = lax.all_to_all(
        jnp.broadcast_to(piece_sum[None], (shards, piece, LANES)), AXES, 0, 0
    ).reshape(packed_shape)

    height = q_rows * q_cols // WIDE + k_rows * k_cols // WIDE
    new_q_master, new_k_master, weights = pl.pallas_call(
        update_kernel,
        in_specs=[smem, smem] + [vmem] * 5,
        out_specs=[vmem] * 3,
        out_shape=[
            jax.ShapeDtypeStruct(q_master.shape, F32),
            jax.ShapeDtypeStruct(k_master.shape, F32),
            jax.ShapeDtypeStruct((height, WIDE), BF16),
        ],
        scratch_shapes=[pltpu.VMEM((2, q_cols, q_cols), BF16)] * 3
        + [pltpu.VMEM((2, k_cols, k_cols), BF16)] * 3,
        compiler_params=pltpu.CompilerParams(vmem_limit_bytes=40 << 20),
    )(block[None], clip_flags, packed, new_q_momentum, new_k_momentum, q_master, k_master)

    gathered = lax.all_to_all(jnp.broadcast_to(weights[None], (16, height, WIDE)), "fsdp", 0, 0)
    thirds = [gathered[:, n * q_rows : (n + 1) * q_rows] for n in range(q_cols // WIDE)]
    after = q_rows * q_cols // WIDE
    halves = [
        gathered[:, after + n * k_rows : after + (n + 1) * k_rows] for n in range(k_cols // WIDE)
    ]
    q_weights = jnp.concatenate(thirds, axis=2).reshape(16 * q_rows, q_cols)
    k_weights = jnp.concatenate(halves, axis=2).reshape(16 * k_rows, k_cols)
    return (new_q_master, new_k_master, new_q_momentum, new_k_momentum, q_weights, k_weights)


def solution(mesh):
    rows = P(AXES, None)
    return jax.shard_map(
        body,
        mesh=mesh,
        in_specs=(rows,) * 9 + (P(),),
        out_specs=(rows,) * 4 + (P("dp", None),) * 2,
        check_vma=False,
    )
```

```python
import functools
import math

import jax
import jax.numpy as jnp
from jax import lax
from jax.experimental import pallas as pl
from jax.experimental.pallas import tpu as pltpu
from jax.sharding import PartitionSpec as P

QNOPE = 128
QROPE = 64
NS_ITERS = 3


COEF_A = 3.4445
COEF_B = -4.775
COEF_C = 2.0315
MOMENTUM_RATE = 0.95
STEP_SIZE = 0.5
DECAY_RATE = 0.1
LOGIT_CAP = 100.0
NORM_EPS = 1e-07

AXES = ("dp", "fsdp")
F32 = jnp.float32
BF16 = jnp.bfloat16
SIZES = {"x": 4, "core": 2, "z": 4, "y": 4}
STRIDES = {"x": 32, "core": 16, "z": 4, "y": 1}
ORDERS = (("x", "z", "y"), ("y", "x", "z"), ("z", "y", "x"))
WIDE = 256
LANES = 128
WIRE_SCALE = 32.0


def hop(array, axis, distance):
    size, stride = SIZES[axis], STRIDES[axis]
    pairs = []
    for source in range(128):
        at = source // stride % size
        pairs.append((source, source + ((at + distance) % size - at) * stride))
    return lax.ppermute(array, AXES, pairs)


def whole(shape):
    return pl.BlockSpec(shape, lambda *_: (0,) * len(shape))


def terms_kernel(position, q_grads, k_grads, q_inputs, k_inputs, zero, one, two):
    contract = (((0,), (0,)), ((), ()))
    q_terms = lax.dot_general(q_grads[...], q_inputs[...], contract, preferred_element_type=F32)
    k_terms = lax.dot_general(k_grads[...], k_inputs[...], contract, preferred_element_type=F32)
    q_rows, k_rows = q_terms.shape[0] // 16, k_terms.shape[0] // 16
    half = k_rows // 2
    for z in range(4):
        for y in range(4):
            to_z, to_y = (z + 4 - position[2]) % 4, (y + 4 - position[3]) % 4
            q_value = q_terms[(z * 4 + y) * q_rows : (z * 4 + y + 1) * q_rows]
            k_value = k_terms[(z * 4 + y) * k_rows : (z * 4 + y + 1) * k_rows]
            one[to_y, 0, to_z, :q_rows] = q_value[:, :WIDE]
            one[to_y, 0, to_z, q_rows:] = k_value[:half, :WIDE]
            two[to_z, to_y, 0, :q_rows] = q_value[:, WIDE : 2 * WIDE]
            two[to_z, to_y, 0, q_rows:] = k_value[half:, :WIDE]
            zero[0, to_z, to_y, :q_rows] = q_value[:, 2 * WIDE :]
            zero[0, to_z, to_y, q_rows:] = k_value[:, WIDE:]


def gradient_terms(position, core_step, q_grads, k_grads, q_inputs, k_inputs):
    tokens = q_grads.shape[0]
    q_slab, k_slab = q_grads.shape[1] // 8, k_grads.shape[1] // 8
    q_rows, k_rows = q_slab // 16, k_slab // 16
    heights = (q_rows + k_rows, q_rows + k_rows // 2, q_rows + k_rows // 2)

    def slab(step, position):
        return (0, (position[0] + step) % 4 * 2 + (position[1] + core_step) % 2)

    q_cols, k_cols = q_inputs.shape[1], k_inputs.shape[1]
    flops = 2 * tokens * 4 * (q_slab * q_cols + k_slab * k_cols)
    moved = 2 * tokens * 4 * (q_slab + k_slab) + 16 * (q_slab * q_cols + k_slab * k_cols)
    return pl.pallas_call(
        terms_kernel,
        grid_spec=pltpu.PrefetchScalarGridSpec(
            num_scalar_prefetch=1,
            grid=(4,),
            in_specs=[
                pl.BlockSpec((tokens, q_slab), slab),
                pl.BlockSpec((tokens, k_slab), slab),
                pl.BlockSpec((tokens, q_cols), lambda step, position: (0, 0)),
                pl.BlockSpec((tokens, k_cols), lambda step, position: (0, 0)),
            ],
            out_specs=[
                pl.BlockSpec(
                    tuple(1 if axis == "x" else 4 for axis in order) + (height, WIDE),
                    lambda step, position, at=order.index("x"): tuple(
                        step if n == at else 0 for n in range(5)
                    ),
                )
                for order, height in zip(ORDERS, heights)
            ],
        ),
        out_shape=[jax.ShapeDtypeStruct((4, 4, 4, height, WIDE), F32) for height in heights],
        cost_estimate=pl.CostEstimate(flops=flops, bytes_accessed=moved, transcendentals=0),
        compiler_params=pltpu.CompilerParams(vmem_limit_bytes=32 << 20),
    )(position, q_grads, k_grads, q_inputs, k_inputs)


def axis_stage(held, stage):
    kept, arrived = [], []
    for color, total in enumerate(held):
        parts = [total[d] for d in range(4)]
        if stage == 0:
            parts[1:] = [(part * WIRE_SCALE).astype(jnp.float16) for part in parts[1:]]
        kept.append(parts[0])
        arrived.append([hop(parts[d], ORDERS[color][stage], d) for d in (1, 2, 3)])
    kept, arrived = lax.optimization_barrier((kept, arrived))
    if stage == 0:
        arrived = [[a.astype(F32) * (1.0 / WIRE_SCALE) for a in parts] for parts in arrived]
    return [[own] + parts for own, parts in zip(kept, arrived)]


def split(value):
    high = value.astype(BF16)
    return high, (value - high.astype(F32)).astype(BF16)


def dot3(first, second, contract=(((1,), (0,)), ((), ()))):
    def one(a, b):
        return lax.dot_general(a, b, contract, preferred_element_type=F32)

    return one(first[0], second[0]) + (one(first[0], second[1]) + one(first[1], second[0]))


def gram_kernel(*refs):
    q_momentum, k_momentum, peaks, new_q, new_k, packed = refs[12:]
    zero, one, two = (
        refs[n][...] + refs[n + 1][...] + refs[n + 2][...] + refs[n + 3][...] for n in (0, 4, 8)
    )
    q_rows, k_rows = q_momentum.shape[0], k_momentum.shape[0]
    half = k_rows // 2
    for n, color in enumerate((one, two, zero)):
        cols = slice(n * WIDE, (n + 1) * WIDE)
        new_q[:, cols] = MOMENTUM_RATE * q_momentum[:, cols] + color[:q_rows]
    new_k[:half, :WIDE] = MOMENTUM_RATE * k_momentum[:half, :WIDE] + one[q_rows:]
    new_k[half:, :WIDE] = MOMENTUM_RATE * k_momentum[half:, :WIDE] + two[q_rows:]
    new_k[:, WIDE:] = MOMENTUM_RATE * k_momentum[:, WIDE:] + zero[q_rows:]
    block = 0
    for moment in (new_q, new_k):
        high, low = split(moment[...])
        count = moment.shape[1] // LANES
        for i in range(count):
            rows = slice(i * LANES, (i + 1) * LANES)
            product = dot3(
                (high[:, rows], low[:, rows]),
                (high[:, i * LANES :], low[:, i * LANES :]),
                (((0,), (0,)), ((), ())),
            )
            for j in range(count - i):
                packed[block] = product[:, j * LANES : (j + 1) * LANES]
                block += 1
    packed[block] = jnp.broadcast_to(peaks[...], (LANES, LANES))


def orthogonal(packed, first, moment, gram, poly, temp):
    size = gram.shape[1]
    count = size // LANES
    trace = jnp.zeros((1, 1), F32)
    diagonal = lax.broadcasted_iota(jnp.int32, (LANES, LANES), 0) == lax.broadcasted_iota(
        jnp.int32, (LANES, LANES), 1
    )
    block = first
    for i in range(count):
        held = jnp.where(diagonal, packed[block], 0.0)
        trace = trace + jnp.sum(jnp.sum(held, axis=1, keepdims=True), axis=0, keepdims=True)
        block += count - i
    scale = 1.0 / (jnp.sqrt(trace) + NORM_EPS)
    square = scale * scale
    block = first
    for i in range(count):
        for j in range(i, count):
            value = packed[block] * square
            block += 1
            rows, cols = slice(i * LANES, (i + 1) * LANES), slice(j * LANES, (j + 1) * LANES)
            gram[0, rows, cols], gram[1, rows, cols] = split(value)
            if j > i:
                gram[0, cols, rows], gram[1, cols, rows] = split(value.T)

    def pair(matrix, cols=slice(None)):
        return matrix[0, :, cols], matrix[1, :, cols]

    def tiles(body):
        def step(index, carry):
            body(pl.ds(pl.multiple_of(index * WIDE, WIDE), WIDE), index * WIDE)
            return carry

        lax.fori_loop(0, size // WIDE, step, 0)

    def polynomial(cols, start):
        held = pair(gram, cols)
        col_ids = lax.broadcasted_iota(jnp.int32, (size, WIDE), 1) + start
        eye = jnp.where(col_ids == lax.broadcasted_iota(jnp.int32, (size, WIDE), 0), COEF_A, 0.0)
        value = held[0].astype(F32) + held[1].astype(F32)
        out = eye + COEF_B * value + COEF_C * dot3(pair(gram), held)
        poly[0, :, cols], poly[1, :, cols] = split(out)

    def gram_poly(cols, start):
        temp[0, :, cols], temp[1, :, cols] = split(dot3(pair(gram), pair(poly, cols)))

    def next_gram(cols, start):
        gram[0, :, cols], gram[1, :, cols] = split(dot3(pair(temp), pair(poly, cols)))

    def times(value, matrix):
        high, low = split(value)
        rows = high.shape[0]
        both = jnp.dot(
            jnp.concatenate((high, low), axis=0), matrix[0], preferred_element_type=F32
        )
        return both[:rows] + (both[rows:] + jnp.dot(high, matrix[1], preferred_element_type=F32))

    current = moment * scale
    tiles(polynomial)
    current = times(current, poly)
    tiles(gram_poly)
    tiles(next_gram)
    tiles(polynomial)
    current = times(current, poly)

    def last_gram(value):
        return times(times(times(value, poly), gram), poly)

    inner = COEF_B * current + COEF_C * last_gram(current)
    return COEF_A * current + last_gram(inner)


def update_kernel(
    place,
    flags,
    packed,
    new_q,
    new_k,
    q_master,
    k_master,
    new_q_master,
    new_k_master,
    weights,
    q_gram,
    q_poly,
    q_temp,
    k_gram,
    k_poly,
    k_temp,
):
    shards = 128
    block = place[0]
    q_rows, k_rows = new_q.shape[0], new_k.shape[0]
    q_blocks = (QNOPE + QROPE) // q_rows
    k_blocks = QNOPE // k_rows
    lane = lax.broadcasted_iota(jnp.int32, (1, LANES), 1)
    peaks = packed[packed.shape[0] - 1, 0:1, :]

    def ratio_of(head):
        peak = jnp.sum(jnp.where(lane == head, peaks, 0.0), axis=1, keepdims=True)
        return jnp.minimum(1.0, LOGIT_CAP / peak)

    q_head, k_head = block // q_blocks, block // k_blocks
    q_ratio, k_ratio = ratio_of(q_head), ratio_of(k_head)
    in_head = block % q_blocks * q_rows + lax.broadcasted_iota(jnp.int32, (q_rows, 1), 0)
    q_factor = jnp.where(in_head < QNOPE, jnp.sqrt(q_ratio), q_ratio)
    q_factor = jnp.where(flags[0, q_head] == 1, q_factor, 1.0)
    k_factor = jnp.where(flags[1, k_head] == 1, jnp.sqrt(k_ratio), 1.0)
    q_gain = 0.2 * math.sqrt(max(shards * q_rows, new_q.shape[1]))
    k_gain = 0.2 * math.sqrt(max(shards * k_rows, new_k.shape[1]))

    count = new_q.shape[1] // LANES
    k_ortho = orthogonal(packed, count * (count + 1) // 2, new_k[...], k_gram, k_poly, k_temp)
    k_out = (k_master[...] - STEP_SIZE * (k_gain * k_ortho + DECAY_RATE * k_master[...])) * k_factor
    new_k_master[...] = k_out
    q_ortho = orthogonal(packed, 0, new_q[...], q_gram, q_poly, q_temp)
    q_out = (q_master[...] - STEP_SIZE * (q_gain * q_ortho + DECAY_RATE * q_master[...])) * q_factor
    new_q_master[...] = q_out
    at = 0
    for value in (q_out, k_out):
        rows = value.shape[0]
        for n in range(value.shape[1] // WIDE):
            weights[at : at + rows] = value[:, n * WIDE : (n + 1) * WIDE].astype(BF16)
            at += rows


def body(
    q_inputs,
    q_grads,
    k_inputs,
    k_grads,
    q_master,
    k_master,
    q_momentum,
    k_momentum,
    logit_peaks,
    clip_flags,
):
    q_rows, q_cols = q_master.shape
    k_rows, k_cols = k_master.shape
    heads = logit_peaks.shape[1]
    dp, fsdp = lax.axis_index("dp"), lax.axis_index("fsdp")
    position = jnp.stack((dp // 2, dp % 2, fsdp // 4, fsdp % 4)).astype(jnp.int32)
    operands = (q_grads, k_grads, q_inputs, k_inputs)

    sent = gradient_terms(position, 1, *operands)
    held = gradient_terms(position, 0, *operands)
    held = [kept + hop(other, "core", 1) for kept, other in zip(held, sent)]
    for stage in range(3):
        held = axis_stage(held, stage)
        if stage < 2:
            held = [own + (one + two + three) for own, one, two, three in held]
    colors = [part for parts in held for part in parts]

    q_count, k_count = q_cols // LANES, k_cols // LANES
    blocks = q_count * (q_count + 1) // 2 + k_count * (k_count + 1) // 2 + 1
    packed_shape = (blocks, LANES, LANES)
    peaks = jnp.pad(logit_peaks, ((0, 0), (0, LANES - heads)))
    smem = pl.BlockSpec(memory_space=pltpu.SMEM)
    vmem = pl.BlockSpec(memory_space=pltpu.VMEM)
    new_q_momentum, new_k_momentum, packed = pl.pallas_call(
        gram_kernel,
        in_specs=[vmem] * 15,
        out_specs=[vmem] * 3,
        out_shape=[
            jax.ShapeDtypeStruct(q_momentum.shape, F32),
            jax.ShapeDtypeStruct(k_momentum.shape, F32),
            jax.ShapeDtypeStruct(packed_shape, F32),
        ],
    )(*colors, q_momentum, k_momentum, peaks)

    shards = 128
    piece = blocks * LANES // shards
    pieces = lax.all_to_all(packed.reshape(shards, piece, LANES), AXES, 0, 0)
    block = dp * 16 + fsdp
    piece_is_peaks = block >= shards - LANES // piece
    piece_sum = jnp.where(piece_is_peaks, jnp.max(pieces, axis=0), jnp.sum(pieces, axis=0))
    packed = lax.all_to_all(
        jnp.broadcast_to(piece_sum[None], (shards, piece, LANES)), AXES, 0, 0
    ).reshape(packed_shape)

    height = q_rows * q_cols // WIDE + k_rows * k_cols // WIDE
    new_q_master, new_k_master, weights = pl.pallas_call(
        update_kernel,
        in_specs=[smem, smem] + [vmem] * 5,
        out_specs=[vmem] * 3,
        out_shape=[
            jax.ShapeDtypeStruct(q_master.shape, F32),
            jax.ShapeDtypeStruct(k_master.shape, F32),
            jax.ShapeDtypeStruct((height, WIDE), BF16),
        ],
        scratch_shapes=[pltpu.VMEM((2, q_cols, q_cols), BF16)] * 3
        + [pltpu.VMEM((2, k_cols, k_cols), BF16)] * 3,
        compiler_params=pltpu.CompilerParams(vmem_limit_bytes=40 << 20),
    )(block[None], clip_flags, packed, new_q_momentum, new_k_momentum, q_master, k_master)

    gathered = lax.all_to_all(jnp.broadcast_to(weights[None], (16, height, WIDE)), "fsdp", 0, 0)
    thirds = [gathered[:, n * q_rows : (n + 1) * q_rows] for n in range(q_cols // WIDE)]
    after = q_rows * q_cols // WIDE
    halves = [
        gathered[:, after + n * k_rows : after + (n + 1) * k_rows] for n in range(k_cols // WIDE)
    ]
    q_weights = jnp.concatenate(thirds, axis=2).reshape(16 * q_rows, q_cols)
    k_weights = jnp.concatenate(halves, axis=2).reshape(16 * k_rows, k_cols)
    return (new_q_master, new_k_master, new_q_momentum, new_k_momentum, q_weights, k_weights)


def solution(mesh):
    rows = P(AXES, None)
    return jax.shard_map(
        body,
        mesh=mesh,
        in_specs=(rows,) * 9 + (P(),),
        out_specs=(rows,) * 4 + (P("dp", None),) * 2,
        check_vma=False,
    )
```
